768 devices in a mesh: users: 192 (over y, z, core), items: 4 (over x).
Axes of the slice: x: 4, y: 8, z: 12, core: 2. Of those that a mesh axis runs over, the one named last changes fastest.
Arguments:
- ratings: bfloat16 [192, 4, 8, 256, 256], P('users', 'items'), may hold values from -6 to 6
- confidence: bfloat16 [192, 4, 8, 256, 256], P('users', 'items'), may hold values from 0 to 2, as said below
- tile_user: int32 [192, 4, 8], P('users', 'items'), may hold values from 0 to 3, as said below
- tile_item: int32 [192, 4, 8], P('users', 'items'), may hold values from 0 to 2, as said below
- tile_count: int32 [192, 4], P('users', 'items'), may hold values from 1 to 8, as said below
- user_factor: bfloat16 [196608, 256], P('users'), may hold values from -1.5 to 1.5
- user_linear: float32 [196608, 256], P('users'), may hold values from -6 to 6
- user_squares: float32 [196608, 256], P('users'), may hold values from 0.25 to 4
- item_factor: bfloat16 [3072, 256], P('items'), may hold values from -1.5 to 1.5
- item_linear: float32 [3072, 256], P('items'), may hold values from -6 to 6
- item_squares: float32 [3072, 256], P('items'), may hold values from 0.25 to 4
Outputs:
- new_user_factor: bfloat16 [196608, 256], P('users')
- new_user_linear: float32 [196608, 256], P('users')
- new_user_squares: float32 [196608, 256], P('users')
- new_item_factor: bfloat16 [3072, 256], P('items')
- new_item_linear: float32 [3072, 256], P('items')
- new_item_squares: float32 [3072, 256], P('items')
The draws below stay inside these ranges and needn't reach their ends.
Inputs may be any that keep to these rules, and one draw needn't show every extreme that they name: Within one device no pair (tile_user, tile_item) occurs twice among its 8 slots. Within one device no pair (tile_user, tile_item) occurs twice among its 8 slots. `tile_count`: some device has all 8 slots live. `confidence`: each entry is zero or at least 0.25.
All inputs are finite; a program needn't handle non-finite values.
Results may differ from the reference program's by a relative error of at most 0.0028.
Values sent between devices are 32-bit elements; how exact they have to be, the bound alone decides.
A program may use at most 32 MiB of HBM per device.

```python
import math
import jax
import jax.numpy as jnp
from jax import lax

R = 256
TILE = 256
TPD = 8
UBD = 4
NIBI = 3
NU = 196608
NI = 3072
N_USERS = 192
N_ITEMS = 4


def tile_pairs(key):
    pair_total = UBD * NIBI
    scores = jax.random.randint(jax.random.fold_in(key, 11), (N_USERS, N_ITEMS, pair_total), 0, 1 << 20)
    scores = scores * pair_total + jnp.arange(pair_total, dtype=jnp.int32)
    ordering = jnp.argsort(scores, axis=-1, stable=True)[..., :TPD]
    return ordering.astype(jnp.int32)


def draw_tile_user(key, part):
    return (tile_pairs(key) // NIBI).astype(jnp.int32)


def draw_tile_item(key, part):
    return (tile_pairs(key) % NIBI).astype(jnp.int32)


def draw_tile_count(key, part):
    draw_one = jax.random.randint(jax.random.fold_in(key, 21), (N_USERS, N_ITEMS), 1, TPD + 1)
    draw_two = jax.random.randint(jax.random.fold_in(key, 22), (N_USERS, N_ITEMS), 1, TPD + 1)
    fewest = jnp.minimum(draw_one, draw_two)
    chosen = jax.random.randint(jax.random.fold_in(key, 23), (), 0, N_USERS * N_ITEMS)
    flat_index = jnp.arange(N_USERS * N_ITEMS, dtype=jnp.int32).reshape(N_USERS, N_ITEMS)
    return jnp.where(flat_index == chosen, TPD, fewest).astype(jnp.int32)


def draw_confidence(key, part):
    conf_shape = (N_USERS, N_ITEMS, TPD, TILE, TILE)
    level_draw = jax.random.uniform(jax.random.fold_in(key, 31), conf_shape, jnp.float32)
    keep_draw = jax.random.randint(jax.random.fold_in(key, 32), conf_shape, 0, 2).astype(jnp.float32)
    return (keep_draw * (0.25 + 1.75 * level_draw)).astype(jnp.bfloat16)


def steps_of(own_key, shape, shards, smallest, top_value):
    def one(position, parts):
        heights = jax.random.uniform(jax.random.fold_in(jax.random.fold_in(own_key, 6), position), (parts,), jnp.float32, smallest / len(shards), top_value / len(shards))
        return jnp.repeat(jnp.exp(heights), shape[position] // parts).reshape((-1,) + (1,) * (len(shape) - position - 1))

    gain = one(*shards[0])
    for cut in shards[1:]:
        gain = gain * one(*cut)
    return gain


def bell_draw(own_key, extent, width, most, split=(), held_as=jnp.bfloat16):
    array = jax.random.normal(own_key, extent, jnp.float32) * width
    if len(split) > 0:
        array = steps_of(own_key, extent, split, -0.22, 0.18) * array
    return jnp.clip(array, min=-most, max=most).astype(held_as)


def setup_inputs(seed: int = 0) -> dict:
    key_list = jax.random.split(jax.random.key(seed), 12)
    ratings = bell_draw(key_list[0], (N_USERS, N_ITEMS, TPD, TILE, TILE), 1.0, 6.0, ((0, 192), (1, 4)))
    confidence = draw_confidence(jax.random.fold_in(key_list[11], 71), 0)
    tile_user = draw_tile_user(jax.random.fold_in(key_list[11], 71), 0)
    tile_item = draw_tile_item(jax.random.fold_in(key_list[11], 71), 0)
    tile_count = draw_tile_count(jax.random.fold_in(key_list[11], 71), 0)
    user_factor = bell_draw(key_list[5], (NU, R), 0.25, 1.5, ((0, 192),))
    user_linear = bell_draw(key_list[6], (NU, R), 1.0, 6.0, ((0, 192),), jnp.float32)
    user_squares = jnp.clip(jnp.exp(math.log(4.0) - 2.7725887 * jax.random.uniform(key_list[7], (NU, R), jnp.float32) ** steps_of(key_list[7], (NU, R), ((0, 192),), -0.2, 0.2)), 0.25, 4.0)
    item_factor = bell_draw(key_list[8], (NI, R), 0.25, 1.5, ((0, 4),))
    item_linear = bell_draw(key_list[9], (NI, R), 1.0, 6.0, ((0, 4),), jnp.float32)
    item_squares = jnp.clip(jnp.exp(math.log(4.0) - 2.7725887 * jax.random.uniform(key_list[10], (NI, R), jnp.float32) ** steps_of(key_list[10], (NI, R), ((0, 4),), -0.2, 0.2)), 0.25, 4.0)
    return {"ratings": ratings, "confidence": confidence, "tile_user": tile_user, "tile_item": tile_item, "tile_count": tile_count, "user_factor": user_factor, "user_linear": user_linear, "user_squares": user_squares, "item_factor": item_factor, "item_linear": item_linear, "item_squares": item_squares}


learn_alpha = 0.25
beta_offset = 1.0
lasso_weight = 0.5
ridge_weight = 1.0

def ftrl_state(gradient, linear, squares, factor):
    new_squares = squares + gradient * gradient
    sigma_step = (jnp.sqrt(new_squares) - jnp.sqrt(squares)) / learn_alpha
    new_linear = linear + gradient - sigma_step * factor.astype(jnp.float32)
    return (new_linear, new_squares)

def ftrl_factor(linear, squares):
    shrink = linear - lasso_weight * jnp.sign(linear)
    denominator = (beta_offset + jnp.sqrt(squares)) / learn_alpha + ridge_weight
    weight = jnp.where(jnp.abs(linear) <= lasso_weight, jnp.zeros_like(linear), -shrink / denominator)
    return weight.astype(jnp.bfloat16)

def reference(ratings, confidence, tile_user, tile_item, tile_count, user_factor, user_linear, user_squares, item_factor, item_linear, item_squares):
    items_four = item_factor.reshape(N_ITEMS, NIBI, TILE, R)
    slot_index = jnp.arange(TPD, dtype=jnp.int32)
    live_mask = (slot_index[None, None, :] < tile_count[:, :, None]).astype(jnp.float32)
    user_pick = (tile_user[..., None] == jnp.arange(UBD, dtype=jnp.int32)).astype(jnp.float32)
    item_pick = (tile_item[..., None] == jnp.arange(NIBI, dtype=jnp.int32)).astype(jnp.float32)
    item_rows = jnp.arange(N_ITEMS, dtype=jnp.int32)[:, None]

    def tile_error(owner, users_four):
        user_tiles = users_four[owner][tile_user[owner]].astype(jnp.float32)
        item_tiles = items_four[item_rows, tile_item[owner]].astype(jnp.float32)
        predict = jnp.einsum('itar,itbr->itab', user_tiles, item_tiles)
        error = live_mask[owner][:, :, None, None] * confidence[owner].astype(jnp.float32) * (predict - ratings[owner].astype(jnp.float32))
        return (error.astype(jnp.bfloat16).astype(jnp.float32), user_tiles, item_tiles)
    users_old = user_factor.reshape(N_USERS, UBD, TILE, R)

    def user_half(owner):
        error, user_tiles, item_tiles = tile_error(owner, users_old)
        per_tile = jnp.einsum('itab,itbr->itar', error, item_tiles)
        return jnp.einsum('itk,itar->kar', user_pick[owner], per_tile, precision=lax.Precision.HIGHEST)
    user_grad = lax.map(user_half, jnp.arange(N_USERS, dtype=jnp.int32)).reshape(NU, R) * TILE ** (-0.5)
    new_user_linear, new_user_squares = ftrl_state(user_grad, user_linear, user_squares, user_factor)
    new_user_factor = ftrl_factor(new_user_linear, new_user_squares)
    users_new = new_user_factor.reshape(N_USERS, UBD, TILE, R)

    def item_half(running_total, owner):
        error, user_tiles, item_tiles = tile_error(owner, users_new)
        per_tile = jnp.einsum('itab,itar->itbr', error, user_tiles)
        return (running_total + jnp.einsum('itk,itbr->ikbr', item_pick[owner], per_tile, precision=lax.Precision.HIGHEST), None)
    start_total = jnp.zeros((N_ITEMS, NIBI, TILE, R), jnp.float32)
    item_total, unused_out = lax.scan(item_half, start_total, jnp.arange(N_USERS, dtype=jnp.int32))
    item_grad = item_total.reshape(NI, R) * (TILE * N_USERS) ** (-0.5)
    new_item_linear, new_item_squares = ftrl_state(item_grad, item_linear, item_squares, item_factor)
    new_item_factor = ftrl_factor(new_item_linear, new_item_squares)
    return (new_user_factor, new_user_linear, new_user_squares, new_item_factor, new_item_linear, new_item_squares)
```

```python
import functools

import jax
import jax.numpy as jnp
from jax import lax
from jax.experimental import pallas as pl
from jax.experimental.pallas import tpu as pltpu
from jax.sharding import PartitionSpec as P

learn_alpha = 0.25
beta_offset = 1.0
lasso_weight = 0.5
ridge_weight = 1.0

ALONG_Z = 12
CORES = 2


def ftrl_state(gradient, linear, squares, factor):
    new_squares = squares + gradient * gradient
    sigma_step = (jnp.sqrt(new_squares) - jnp.sqrt(squares)) / learn_alpha
    new_linear = linear + gradient - sigma_step * factor.astype(jnp.float32)
    return (new_linear, new_squares)


def ftrl_factor(linear, squares):
    shrink = linear - lasso_weight * jnp.sign(linear)
    denominator = (beta_offset + jnp.sqrt(squares)) / learn_alpha + ridge_weight
    weight = jnp.where(
        jnp.abs(linear) <= lasso_weight, jnp.zeros_like(linear), -shrink / denominator
    )
    return weight.astype(jnp.bfloat16)


def slot_table(tile_user, tile_item, item_blocks):
    return [tile_user[t] * item_blocks + tile_item[t] for t in range(tile_user.shape[0])]


def slot_of(codes, count, pair):
    slot = jnp.int32(0)
    live = jnp.int32(0)
    for t, code in enumerate(codes):
        slot = jnp.where(code == pair, t, slot)
        live = jnp.where(code == pair, jnp.where(t < count, 1, 0), live)
    return slot, live.astype(jnp.float32)


def pair_error(user_rows, item_rows, ratings, confidence, live):
    predict = lax.dot_general(
        user_rows, item_rows, (((1,), (1,)), ((), ())), preferred_element_type=jnp.float32
    )
    error = live * confidence.astype(jnp.float32) * (predict - ratings.astype(jnp.float32))
    return error.astype(jnp.bfloat16)


def remote(source, target, send, receive, device):
    return pltpu.make_async_remote_copy(
        src_ref=source,
        dst_ref=target,
        send_sem=send,
        recv_sem=receive,
        device_id=device,
        device_id_type=pl.DeviceIdType.MESH,
    )


def user_kernel(
    tile_user,
    tile_item,
    tile_count,
    ratings,
    confidence,
    user_factor,
    item_factor,
    total,
    part,
    pass_right,
    pass_left,
    from_left,
    from_right,
    send,
    receive,
):
    user_blocks, width, rank = user_factor.shape
    item_blocks = item_factor.shape[0]
    half = width // 2
    n = lax.axis_size("items")
    me = lax.axis_index("items")
    right, left, far = lax.rem(me + 1, n), lax.rem(me + 3, n), lax.rem(me + 2, n)

    barrier = pltpu.get_barrier_semaphore()
    for other in (left, right):
        pl.semaphore_signal(
            barrier, inc=1, device_id={"items": other}, device_id_type=pl.DeviceIdType.MESH
        )

    codes = slot_table(tile_user, tile_item, item_blocks)
    count = tile_count[0]

    def block(k):
        rows = user_factor[k]
        gradient = jnp.zeros((width, rank), jnp.float32)
        for i in range(item_blocks):
            slot, live = slot_of(codes, count, k * item_blocks + i)
            error = pair_error(rows, item_factor[i], ratings[slot], confidence[slot], live)
            gradient += jnp.dot(error, item_factor[i], preferred_element_type=jnp.float32)
        part[k] = gradient

    low, high = pl.ds(0, half), pl.ds(half, half)

    block(far)
    pl.semaphore_wait(barrier, 2)
    copies = [
        remote(part.at[far, low], pass_right, send.at[0], receive.at[0], {"items": right}),
        remote(part.at[far, high], pass_left, send.at[1], receive.at[1], {"items": left}),
        remote(part.at[right, high], from_left.at[high], send.at[2], receive.at[2], {"items": right}),
        remote(part.at[left, low], from_right.at[low], send.at[3], receive.at[3], {"items": left}),
        remote(part.at[right, low], from_left.at[low], send.at[4], receive.at[4], {"items": right}),
        remote(part.at[left, high], from_right.at[high], send.at[5], receive.at[5], {"items": left}),
        remote(total.at[me, low], total.at[me, low], send.at[6], receive.at[6], {"items": right}),
        remote(total.at[me, high], total.at[me, high], send.at[7], receive.at[7], {"items": left}),
        remote(total.at[me, high], total.at[me, high], send.at[8], receive.at[8], {"items": right}),
        remote(total.at[me, low], total.at[me, low], send.at[9], receive.at[9], {"items": left}),
        remote(total.at[left, low], total.at[left, low], send.at[10], receive.at[10], {"items": right}),
        remote(total.at[right, high], total.at[right, high], send.at[11], receive.at[11], {"items": left}),
    ]
    copies[0].start()
    copies[1].start()
    block(right)
    copies[2].start()
    block(left)
    copies[3].start()
    copies[0].wait_recv()
    part[right, low] += pass_right[...]
    copies[1].wait_recv()
    part[left, high] += pass_left[...]
    copies[4].start()
    copies[5].start()
    block(me)
    copies[3].wait_recv()
    copies[4].wait_recv()
    total[me, low] = part[me, low] + (from_left[low] + from_right[low])
    copies[6].start()
    copies[2].wait_recv()
    copies[5].wait_recv()
    total[me, high] = part[me, high] + (from_left[high] + from_right[high])
    copies[7].start()
    copies[8].start()
    copies[9].start()
    copies[6].wait_recv()
    copies[10].start()
    copies[7].wait_recv()
    copies[11].start()
    for j in range(8, 12):
        copies[j].wait_recv()
    for j in range(12):
        copies[j].wait_send()


def item_kernel(
    along_z,
    tile_user,
    tile_item,
    tile_count,
    ratings,
    confidence,
    user_factor,
    item_factor,
    total,
    part,
    arrived,
    mine,
    chunk_sum,
    first_in,
    second_in,
    pair_sem,
    send_first,
    recv_first,
    send_second,
    recv_second,
    send_tile,
    recv_tile,
    send_chunk,
    recv_chunk,
    send_over,
    recv_over,
):
    user_blocks, width, rank = user_factor.shape
    item_blocks = item_factor.shape[0]
    half_rows = item_blocks * width // CORES
    along_y = lax.axis_size("users") // (along_z * CORES)
    me = lax.axis_index("users")
    core = lax.rem(me, CORES)
    z = lax.rem(me // CORES, along_z)
    y = me // (CORES * along_z)
    partner = me + 1 - 2 * core

    def at_y(t):
        return {"users": (t * along_z + z) * CORES + core}

    def at_z(t):
        return {"users": (y * along_z + t) * CORES + core}

    def greet(device):
        pl.semaphore_signal(
            barrier, inc=1, device_id=device, device_id_type=pl.DeviceIdType.MESH
        )

    barrier = pltpu.get_barrier_semaphore()
    greet({"users": partner})

    @pl.loop(1, along_y)
    def _(d):
        greet(at_y(lax.rem(y + d, along_y)))

    @pl.loop(1, along_z)
    def _(d):
        greet(at_z(lax.rem(z + d, along_z)))

    codes = slot_table(tile_user, tile_item, item_blocks)
    count = tile_count[0]

    def block(i):
        rows = item_factor[i]
        gradient = jnp.zeros((width, rank), jnp.float32)
        for k in range(user_blocks):
            slot, live = slot_of(codes, count, k * item_blocks + i)
            error = pair_error(user_factor[k], rows, ratings[slot], confidence[slot], live)
            gradient += lax.dot_general(
                error,
                user_factor[k],
                (((0,), (0,)), ((), ())),
                preferred_element_type=jnp.float32,
            )
        part[pl.ds(pl.multiple_of(i * width, width), width), :] = gradient

    own = pl.ds(pl.multiple_of(core * half_rows, half_rows), half_rows)
    theirs = pl.ds(pl.multiple_of((1 - core) * half_rows, half_rows), half_rows)
    block((item_blocks - 1) * (1 - core))
    block(1)
    pl.semaphore_wait(barrier, along_y + along_z - 1)
    swap = remote(part.at[theirs], arrived, pair_sem.at[0], pair_sem.at[1], {"users": partner})
    swap.start()
    block((item_blocks - 1) * core)
    swap.wait_recv()
    mine[...] = part[own, :] + arrived[...]

    def halves(base, n_first, first, at_first, n_second, second, at_second):
        chunk = half_rows // n_first

        def distance(n, j):
            step = (j + 1) // 2
            return n // 2 + step * (1 - 2 * lax.rem(j, 2))

        def rows_of(t):
            return pl.ds(pl.multiple_of(t * chunk, chunk), chunk)

        def out_rows(t):
            return pl.ds(pl.multiple_of(base + t * chunk, 8), chunk)

        def tile_of(t, start):
            return (
                pl.ds(pl.multiple_of(start + 8 * (t // 2), 8), 8),
                pl.ds(pl.multiple_of(128 * lax.rem(t, 2), 128), 128),
            )

        def to_first(j):
            t = lax.rem(first + distance(n_first, j), n_first)
            return remote(
                mine.at[rows_of(t)],
                first_in.at[j, pl.ds(0, chunk)],
                send_first.at[j],
                recv_first.at[j],
                at_first(t),
            )

        def to_second(j):
            t = lax.rem(second + distance(n_second, j), n_second)
            return remote(
                chunk_sum.at[tile_of(t, 0)],
                second_in.at[j],
                send_second.at[j],
                recv_second.at[j],
                at_second(t),
            )

        my_tile = tile_of(second, base + first * chunk)

        def tile_out(j):
            t = lax.rem(second + distance(n_second, j), n_second)
            return remote(
                total.at[my_tile], total.at[my_tile], send_tile.at[j], recv_tile.at[j], at_second(t)
            )

        def chunk_out(j):
            t = lax.rem(first + distance(n_first, j), n_first)
            return remote(
                total.at[out_rows(first)],
                total.at[out_rows(first)],
                send_chunk.at[j],
                recv_chunk.at[j],
                at_first(t),
            )

        def over(slot, t):
            return remote(
                total.at[out_rows(t)],
                total.at[out_rows(t)],
                send_over.at[slot],
                recv_over.at[slot],
                {"users": partner},
            )

        @pl.loop(0, n_first - 1)
        def _(j):
            to_first(j).start()

        def add_first(j, running):
            to_first(j).wait_recv()
            return running + first_in[j, pl.ds(0, chunk), :]

        chunk_sum[pl.ds(0, chunk), :] = lax.fori_loop(
            0, n_first - 1, add_first, mine[rows_of(first), :]
        )

        @pl.loop(0, n_second - 1)
        def _(j):
            to_second(j).start()

        def add_second(j, running):
            to_second(j).wait_recv()
            return running + second_in[j]

        total[my_tile] = lax.fori_loop(
            0, n_second - 1, add_second, chunk_sum[tile_of(second, 0)]
        )

        @pl.loop(0, n_second - 1)
        def _(j):
            tile_out(j).start()

        @pl.loop(0, n_second - 1)
        def _(j):
            tile_out(j).wait_recv()

        @pl.loop(0, n_first - 1)
        def _(j):
            chunk_out(j).start()

        over(n_first - 1, first).start()

        @pl.loop(0, n_first - 1)
        def _(j):
            chunk_out(j).wait_recv()
            over(j, lax.rem(first + n_first - distance(n_first, j), n_first)).start()

        @pl.loop(0, n_first - 1)
        def _(j):
            to_first(j).wait_send()
            chunk_out(j).wait_send()

        @pl.loop(0, n_second - 1)
        def _(j):
            to_second(j).wait_send()
            tile_out(j).wait_send()

        @pl.loop(0, n_first)
        def _(j):
            over(j, 0).wait_send()

        other_chunk = half_rows // n_second

        @pl.loop(0, n_second)
        def _(j):
            remote(
                total.at[pl.ds(0, other_chunk)],
                total.at[pl.ds(0, other_chunk)],
                send_over.at[j],
                recv_over.at[j],
                {"users": partner},
            ).wait_recv()

    @pl.when(core == 0)
    def _():
        halves(0, along_y, y, at_y, along_z, z, at_z)

    @pl.when(core == 1)
    def _():
        halves(half_rows, along_z, z, at_z, along_y, y, at_y)

    swap.wait_send()


VMEM = pl.BlockSpec(memory_space=pltpu.VMEM)
SMEM = pl.BlockSpec(memory_space=pltpu.SMEM)
IN_SPECS = [SMEM, SMEM, SMEM, VMEM, VMEM, VMEM, VMEM]
DMA = pltpu.SemaphoreType.DMA


def user_total(tiles, user_factor, item_factor):
    blocks, width, rank = user_factor.shape
    half = (width // 2, rank)
    return pl.pallas_call(
        user_kernel,
        name="user_total",
        out_shape=jax.ShapeDtypeStruct((blocks, width, rank), jnp.float32),
        in_specs=IN_SPECS,
        out_specs=VMEM,
        scratch_shapes=[
            pltpu.VMEM((blocks, width, rank), jnp.float32),
            pltpu.VMEM(half, jnp.float32),
            pltpu.VMEM(half, jnp.float32),
            pltpu.VMEM((width, rank), jnp.float32),
            pltpu.VMEM((width, rank), jnp.float32),
            DMA((12,)),
            DMA((12,)),
        ],
        compiler_params=pltpu.CompilerParams(
            collective_id=0, has_side_effects=True, vmem_limit_bytes=48 << 20
        ),
    )(*tiles, user_factor, item_factor)


def item_total(tiles, user_factor, item_factor, along_y, along_z):
    blocks, width, rank = item_factor.shape
    rows = blocks * width
    half_rows = rows // CORES
    most = max(along_y, along_z)
    chunk = half_rows // min(along_y, along_z)
    return pl.pallas_call(
        functools.partial(item_kernel, along_z),
        name="item_total",
        out_shape=jax.ShapeDtypeStruct((rows, rank), jnp.float32),
        in_specs=IN_SPECS,
        out_specs=VMEM,
        scratch_shapes=[
            pltpu.VMEM((rows, rank), jnp.float32),
            pltpu.VMEM((half_rows, rank), jnp.float32),
            pltpu.VMEM((half_rows, rank), jnp.float32),
            pltpu.VMEM((chunk, rank), jnp.float32),
            pltpu.VMEM((most - 1, chunk, rank), jnp.float32),
            pltpu.VMEM((most - 1, 8, 128), jnp.float32),
            DMA((2,)),
        ]
        + [DMA((most,))] * 10,
        compiler_params=pltpu.CompilerParams(
            collective_id=1, has_side_effects=True, vmem_limit_bytes=48 << 20
        ),
    )(*tiles, user_factor, item_factor)


def on_device(
    ratings,
    confidence,
    tile_user,
    tile_item,
    tile_count,
    user_factor,
    user_linear,
    user_squares,
    item_factor,
    item_linear,
    item_squares,
):
    slot_count = ratings.shape[2]
    width = ratings.shape[3]
    rank = user_factor.shape[1]
    user_blocks = user_factor.shape[0] // width
    item_blocks = item_factor.shape[0] // width
    user_devices = lax.axis_size("users")
    tiles = (
        tile_user.reshape(slot_count),
        tile_item.reshape(slot_count),
        tile_count.reshape(1),
        ratings.reshape(slot_count, width, width),
        confidence.reshape(slot_count, width, width),
    )
    items = item_factor.reshape(item_blocks, width, rank)
    user_sum = user_total(tiles, user_factor.reshape(user_blocks, width, rank), items)
    user_grad = user_sum.reshape(user_blocks * width, rank) * width ** (-0.5)
    new_user_linear, new_user_squares = ftrl_state(
        user_grad, user_linear, user_squares, user_factor
    )
    new_user_factor = ftrl_factor(new_user_linear, new_user_squares)
    item_sum = item_total(
        tiles,
        new_user_factor.reshape(user_blocks, width, rank),
        items,
        user_devices // (ALONG_Z * CORES),
        ALONG_Z,
    )
    item_grad = item_sum * (width * user_devices) ** (-0.5)
    new_item_linear, new_item_squares = ftrl_state(
        item_grad, item_linear, item_squares, item_factor
    )
    new_item_factor = ftrl_factor(new_item_linear, new_item_squares)
    return (
        new_user_factor,
        new_user_linear,
        new_user_squares,
        new_item_factor,
        new_item_linear,
        new_item_squares,
    )


def solution(mesh):
    placed = (
        P("users", "items", None, None, None),
        P("users", "items", None, None, None),
        P("users", "items", None),
        P("users", "items", None),
        P("users", "items"),
        P("users", None),
        P("users", None),
        P("users", None),
        P("items", None),
        P("items", None),
        P("items", None),
    )
    return jax.shard_map(
        on_device,
        mesh=mesh,
        in_specs=placed,
        out_specs=(
            P("users", None),
            P("users", None),
            P("users", None),
            P("items", None),
            P("items", None),
            P("items", None),
        ),
        check_vma=False,
    )
```

```python
import functools

import jax
import jax.numpy as jnp
from jax import lax
from jax.experimental import pallas as pl
from jax.experimental.pallas import tpu as pltpu
from jax.sharding import PartitionSpec as P

learn_alpha = 0.25
beta_offset = 1.0
lasso_weight = 0.5
ridge_weight = 1.0

ALONG_Z = 12
CORES = 2


def ftrl_state(gradient, linear, squares, factor):
    new_squares = squares + gradient * gradient
    sigma_step = (jnp.sqrt(new_squares) - jnp.sqrt(squares)) / learn_alpha
    new_linear = linear + gradient - sigma_step * factor.astype(jnp.float32)
    return (new_linear, new_squares)


def ftrl_factor(linear, squares):
    shrink = linear - lasso_weight * jnp.sign(linear)
    denominator = (beta_offset + jnp.sqrt(squares)) / learn_alpha + ridge_weight
    weight = jnp.where(
        jnp.abs(linear) <= lasso_weight, jnp.zeros_like(linear), -shrink / denominator
    )
    return weight.astype(jnp.bfloat16)


def slot_table(tile_user, tile_item, item_blocks):
    return [tile_user[t] * item_blocks + tile_item[t] for t in range(tile_user.shape[0])]


def slot_of(codes, count, pair):
    slot = jnp.int32(0)
    live = jnp.int32(0)
    for t, code in enumerate(codes):
        slot = jnp.where(code == pair, t, slot)
        live = jnp.where(code == pair, jnp.where(t < count, 1, 0), live)
    return slot, live.astype(jnp.float32)


def pair_error(user_rows, item_rows, ratings, confidence, live):
    predict = lax.dot_general(
        user_rows, item_rows, (((1,), (1,)), ((), ())), preferred_element_type=jnp.float32
    )
    error = live * confidence.astype(jnp.float32) * (predict - ratings.astype(jnp.float32))
    return error.astype(jnp.bfloat16)


def remote(source, target, send, receive, device):
    return pltpu.make_async_remote_copy(
        src_ref=source,
        dst_ref=target,
        send_sem=send,
        recv_sem=receive,
        device_id=device,
        device_id_type=pl.DeviceIdType.MESH,
    )


def both_kernel(
    along_z,
    user_scale,
    tile_user,
    tile_item,
    tile_count,
    ratings_hbm,
    confidence_hbm,
    linear_hbm,
    squares_hbm,
    user_factor,
    item_factor,
    user_out,
    total,
    ratings,
    confidence,
    linear,
    squares,
    user_part,
    user_sum,
    fresh,
    pass_right,
    pass_left,
    from_left,
    from_right,
    part,
    arrived,
    mine,
    chunk_sum,
    first_in,
    tile_in,
    whole_in,
    load_sem,
    user_send,
    user_recv,
    send_swap,
    recv_swap,
    send_first,
    recv_first,
    send_second,
    recv_second,
    send_tile,
    recv_tile,
    send_chunk,
    recv_chunk,
    send_over,
    recv_over,
):
    user_blocks, width, rank = user_factor.shape
    item_blocks = item_factor.shape[0]
    half = width // 2
    quarter = width // 4
    half_rows = item_blocks * width // CORES
    along_y = lax.axis_size("users") // (along_z * CORES)
    user = lax.axis_index("users")
    core = lax.rem(user, CORES)
    z = lax.rem(user // CORES, along_z)
    y = user // (CORES * along_z)
    partner = {"users": user + 1 - 2 * core}
    n = lax.axis_size("items")
    me = lax.axis_index("items")
    right, left, far = lax.rem(me + 1, n), lax.rem(me + 3, n), lax.rem(me + 2, n)

    def at_y(t):
        return {"users": (t * along_z + z) * CORES + core}

    def at_z(t):
        return {"users": (y * along_z + t) * CORES + core}

    def greet(device):
        pl.semaphore_signal(
            barrier, inc=1, device_id=device, device_id_type=pl.DeviceIdType.MESH
        )

    barrier = pltpu.get_barrier_semaphore()
    loads = [
        pltpu.make_async_copy(ratings_hbm, ratings, load_sem.at[0]),
        pltpu.make_async_copy(confidence_hbm, confidence, load_sem.at[1]),
        pltpu.make_async_copy(linear_hbm, linear, load_sem.at[2]),
        pltpu.make_async_copy(squares_hbm, squares, load_sem.at[3]),
    ]
    loads[0].start()
    loads[1].start()
    greet({"items": left})
    greet({"items": right})
    greet(partner)

    @pl.loop(1, along_y)
    def _(d):
        greet(at_y(lax.rem(y + d, along_y)))

    @pl.loop(1, along_z)
    def _(d):
        greet(at_z(lax.rem(z + d, along_z)))

    codes = slot_table(tile_user, tile_item, item_blocks)
    count = tile_count[0]

    def user_block(k):
        rows = user_factor[k]
        gradient = jnp.zeros((width, rank), jnp.float32)
        for i in range(item_blocks):
            slot, live = slot_of(codes, count, k * item_blocks + i)
            error = pair_error(rows, item_factor[i], ratings[slot], confidence[slot], live)
            gradient += jnp.dot(error, item_factor[i], preferred_element_type=jnp.float32)
        user_part[k] = gradient

    def rows_at(start, size):
        return pl.ds(start, size)

    low, high = rows_at(0, half), rows_at(half, half)
    fours = [rows_at(q * quarter, quarter) for q in range(4)]
    to_right, to_left = {"items": right}, {"items": left}

    def user_copy(j, source, target, device):
        return remote(source, target, user_send.at[j], user_recv.at[j], device)

    far_right = user_copy(0, user_part.at[far, low], pass_right, to_right)
    far_left = user_copy(1, user_part.at[far, high], pass_left, to_left)
    near_right = user_copy(2, user_part.at[right, high], from_left.at[high], to_right)
    near_left = user_copy(3, user_part.at[left, low], from_right.at[low], to_left)
    sums_right = [
        user_copy(4 + q, user_part.at[right, fours[q]], from_left.at[fours[q]], to_right)
        for q in range(2)
    ]
    sums_left = [
        user_copy(4 + q, user_part.at[left, fours[q]], from_right.at[fours[q]], to_left)
        for q in range(2, 4)
    ]
    own_right = [
        user_copy(8 + q, user_sum.at[me, fours[q]], user_sum.at[me, fours[q]], to_right)
        for q in range(4)
    ]
    own_left = [
        user_copy(12 + q, user_sum.at[me, fours[q]], user_sum.at[me, fours[q]], to_left)
        for q in range(4)
    ]
    on_right = [
        user_copy(16 + q, user_sum.at[left, fours[q]], user_sum.at[left, fours[q]], to_right)
        for q in range(2)
    ]
    on_left = [
        user_copy(16 + q, user_sum.at[right, fours[q]], user_sum.at[right, fours[q]], to_left)
        for q in range(2, 4)
    ]

    loads[0].wait()
    loads[1].wait()
    loads[2].start()
    loads[3].start()
    user_block(far)
    pl.semaphore_wait(barrier, along_y + along_z + 1)
    far_right.start()
    far_left.start()
    user_block(right)
    near_right.start()
    user_block(left)
    near_left.start()
    far_right.wait_recv()
    for q in range(2):
        user_part[right, fours[q]] += pass_right[fours[q]]
        sums_right[q].start()
    far_left.wait_recv()
    for q in range(2, 4):
        user_part[left, fours[q]] += pass_left[fours[q - 2]]
        sums_left[q - 2].start()
    user_block(me)

    def own_sum(q):
        user_sum[me, fours[q]] = user_part[me, fours[q]] + (
            from_left[fours[q]] + from_right[fours[q]]
        )

    near_left.wait_recv()
    near_right.wait_recv()
    for q in range(2):
        sums_right[q].wait_recv()
        own_sum(q)
        own_right[q].start()
        sums_left[q].wait_recv()
        own_sum(2 + q)
        own_left[2 + q].start()
    for q in range(2):
        own_right[2 + q].start()
        own_left[q].start()
    loads[2].wait()
    loads[3].wait()

    def new_factor(k, start):
        slab = min(32, half)

        @pl.loop(0, half // slab)
        def _(j):
            rows = pl.ds(pl.multiple_of(start + j * slab, slab), slab)
            gradient = user_sum[k, rows, :] * user_scale
            state, spread = ftrl_state(
                gradient, linear[k, rows, :], squares[k, rows, :], user_factor[k, rows, :]
            )
            shrink = state - jnp.where(state > 0.0, lasso_weight, -lasso_weight)
            denominator = (beta_offset + jnp.sqrt(spread)) / learn_alpha + ridge_weight
            weight = jnp.where(
                jnp.abs(state) <= lasso_weight, jnp.zeros_like(state), -shrink / denominator
            )
            fresh[k, rows, :] = weight.astype(jnp.bfloat16)

    def item_block(k, i, first=False):
        rows = pl.ds(pl.multiple_of(i * width, width), width)
        slot, live = slot_of(codes, count, k * item_blocks + i)
        error = pair_error(fresh[k], item_factor[i], ratings[slot], confidence[slot], live)
        gradient = lax.dot_general(
            error, fresh[k], (((0,), (0,)), ((), ())), preferred_element_type=jnp.float32
        )
        if first:
            part[rows, :] = gradient
        else:
            part[rows, :] += gradient

    new_factor(me, 0)
    new_factor(me, half)
    for q in range(2):
        own_right[q].wait_recv()
        on_right[q].start()
        own_left[2 + q].wait_recv()
        on_left[q].start()
    for i in range(item_blocks):
        item_block(me, i, first=True)
    new_factor(left, 0)
    new_factor(right, half)
    own_right[2].wait_recv()
    own_right[3].wait_recv()
    new_factor(left, half)
    for i in range(item_blocks):
        item_block(left, i)
    own_left[0].wait_recv()
    own_left[1].wait_recv()
    new_factor(right, 0)
    for i in range(item_blocks):
        item_block(right, i)
    for copy in on_right:
        copy.wait_recv()
    new_factor(far, 0)
    for copy in on_left:
        copy.wait_recv()
    new_factor(far, half)
    store = pltpu.make_async_copy(user_sum, user_out, load_sem.at[4])
    store.start()
    item_block(far, (item_blocks - 1) * (1 - core))
    item_block(far, 1)

    def distance(count, j):
        step = (j + 1) // 2
        return count // 2 + step * (1 - 2 * lax.rem(j, 2))

    def swaps(base, count, place):
        chunk = half_rows // count

        def one(j):
            t = lax.rem(place + distance(count, j), count)
            return remote(
                part.at[pl.ds(pl.multiple_of(base + t * chunk, 8), chunk)],
                arrived.at[pl.ds(pl.multiple_of(t * chunk, 8), chunk)],
                send_swap.at[j],
                recv_swap.at[j],
                partner,
            )

        return one

    def halves(other, base, n_first, first, at_first, n_second, second, at_second, direct):
        chunk = half_rows // n_first
        to_partner = swaps(other, n_second, second)
        from_partner = swaps(base, n_first, first)

        @pl.loop(0, n_second)
        def _(j):
            to_partner(j).start()

        item_block(far, (item_blocks - 1) * (base // half_rows))

        def rows_of(t):
            return pl.ds(pl.multiple_of(t * chunk, 8), chunk)

        def out_rows(t):
            return pl.ds(pl.multiple_of(base + t * chunk, 8), chunk)

        def tile_of(t, start):
            return (
                pl.ds(pl.multiple_of(start + 8 * (t // 2), 8), 8),
                pl.ds(pl.multiple_of(128 * lax.rem(t, 2), 128), 128),
            )

        def first_target(j):
            return lax.rem(first + distance(n_first, j), n_first)

        def second_target(j):
            return lax.rem(second + distance(n_second, j), n_second)

        def to_first(j):
            t = first_target(j)
            return remote(
                mine.at[rows_of(t)],
                first_in.at[j, pl.ds(0, chunk)],
                send_first.at[j],
                recv_first.at[j],
                at_first(t),
            )

        def to_second(j):
            t = second_target(j)
            return remote(
                chunk_sum.at[tile_of(t, 0)],
                tile_in.at[j],
                send_second.at[j],
                recv_second.at[j],
                at_second(t),
            )

        def whole_to(j):
            return remote(
                whole_in.at[second],
                whole_in.at[second],
                send_second.at[j],
                recv_second.at[j],
                at_second(second_target(j)),
            )

        my_tile = tile_of(second, base + first * chunk)

        def tile_out(j):
            return remote(
                total.at[my_tile],
                total.at[my_tile],
                send_tile.at[j],
                recv_tile.at[j],
                at_second(second_target(j)),
            )

        def chunk_out(j):
            return remote(
                total.at[out_rows(first)],
                total.at[out_rows(first)],
                send_chunk.at[j],
                recv_chunk.at[j],
                at_first(first_target(j)),
            )

        def over(slot, t):
            return remote(
                total.at[out_rows(t)],
                total.at[out_rows(t)],
                send_over.at[slot],
                recv_over.at[slot],
                partner,
            )

        @pl.loop(0, n_first - 1)
        def _(j):
            t = first_target(j)
            from_partner(j).wait_recv()
            mine[rows_of(t), :] = part[out_rows(t), :] + arrived[rows_of(t), :]
            to_first(j).start()

        from_partner(n_first - 1).wait_recv()

        def add_first(j, running):
            to_first(j).wait_recv()
            return running + first_in[j, pl.ds(0, chunk), :]

        near = lax.fori_loop(
            0,
            n_first - 1,
            add_first,
            part[out_rows(first), :] + arrived[rows_of(first), :],
        )

        if direct:
            whole_in[second] = near

            @pl.loop(0, n_second - 1)
            def _(j):
                whole_to(j).start()

            @pl.loop(0, n_second - 1)
            def _(j):
                whole_to(j).wait_recv()

            total[out_rows(first), :] = lax.fori_loop(
                1, n_second, lambda j, running: running + whole_in[j], whole_in[0]
            )
        else:
            chunk_sum[...] = near

            @pl.loop(0, n_second - 1)
            def _(j):
                to_second(j).start()

            def add_second(j, running):
                to_second(j).wait_recv()
                return running + tile_in[j]

            total[my_tile] = lax.fori_loop(
                0, n_second - 1, add_second, chunk_sum[tile_of(second, 0)]
            )

            @pl.loop(0, n_second - 1)
            def _(j):
                tile_out(j).start()

            @pl.loop(0, n_second - 1)
            def _(j):
                tile_out(j).wait_recv()

        @pl.loop(0, n_first - 1)
        def _(j):
            chunk_out(j).start()

        over(n_first - 1, first).start()

        @pl.loop(0, n_first - 1)
        def _(j):
            chunk_out(j).wait_recv()
            over(j, lax.rem(first + n_first - distance(n_first, j), n_first)).start()

        @pl.loop(0, n_first - 1)
        def _(j):
            to_first(j).wait_send()
            chunk_out(j).wait_send()

        @pl.loop(0, n_second - 1)
        def _(j):
            if direct:
                whole_to(j).wait_send()
            else:
                to_second(j).wait_send()
                tile_out(j).wait_send()

        @pl.loop(0, n_first)
        def _(j):
            over(j, 0).wait_send()

        @pl.loop(0, n_second)
        def _(j):
            to_partner(j).wait_send()

        other_chunk = half_rows // n_second

        @pl.loop(0, n_second)
        def _(j):
            remote(
                total.at[pl.ds(0, other_chunk)],
                total.at[pl.ds(0, other_chunk)],
                send_over.at[j],
                recv_over.at[j],
                partner,
            ).wait_recv()

    @pl.when(core == 0)
    def _():
        halves(half_rows, 0, along_y, y, at_y, along_z, z, at_z, False)

    @pl.when(core == 1)
    def _():
        halves(0, half_rows, along_z, z, at_z, along_y, y, at_y, True)

    for copy in [far_right, far_left, near_right, near_left] + sums_right + sums_left:
        copy.wait_send()
    for copy in own_right + own_left + on_right + on_left:
        copy.wait_send()
    store.wait()


VMEM = pl.BlockSpec(memory_space=pltpu.VMEM)
SMEM = pl.BlockSpec(memory_space=pltpu.SMEM)
ANY = pl.BlockSpec(memory_space=pl.ANY)
DMA = pltpu.SemaphoreType.DMA


def both_totals(tiles, linear, squares, user_factor, item_factor, along_y, along_z):
    blocks, width, rank = user_factor.shape
    rows = item_factor.shape[0] * width
    half_rows = rows // CORES
    most = max(along_y, along_z)
    chunk_y, chunk_z = half_rows // along_y, half_rows // along_z
    chunk = max(chunk_y, chunk_z)
    f32 = jnp.float32
    whole = (blocks, width, rank)
    return pl.pallas_call(
        functools.partial(both_kernel, along_z, width ** (-0.5)),
        name="both_totals",
        out_shape=(jax.ShapeDtypeStruct(whole, f32), jax.ShapeDtypeStruct((rows, rank), f32)),
        in_specs=[SMEM] * 3 + [ANY] * 4 + [VMEM] * 2,
        out_specs=(ANY, VMEM),
        scratch_shapes=[
            pltpu.VMEM(tiles[3].shape, tiles[3].dtype),
            pltpu.VMEM(tiles[4].shape, tiles[4].dtype),
            pltpu.VMEM(whole, f32),
            pltpu.VMEM(whole, f32),
            pltpu.VMEM(whole, f32),
            pltpu.VMEM(whole, f32),
            pltpu.VMEM(whole, user_factor.dtype),
            pltpu.VMEM((width // 2, rank), f32),
            pltpu.VMEM((width // 2, rank), f32),
            pltpu.VMEM((width, rank), f32),
            pltpu.VMEM((width, rank), f32),
            pltpu.VMEM((rows, rank), f32),
            pltpu.VMEM((half_rows, rank), f32),
            pltpu.VMEM((half_rows, rank), f32),
            pltpu.VMEM((chunk_y, rank), f32),
            pltpu.VMEM((most - 1, chunk, rank), f32),
            pltpu.VMEM((most - 1, 8, 128), f32),
            pltpu.VMEM((along_y, chunk_z, rank), f32),
            DMA((5,)),
            DMA((20,)),
            DMA((20,)),
        ]
        + [DMA((most,))] * 12,
        compiler_params=pltpu.CompilerParams(collective_id=0, has_side_effects=True),
    )(*tiles, linear, squares, user_factor, item_factor)


def on_device(
    ratings,
    confidence,
    tile_user,
    tile_item,
    tile_count,
    user_factor,
    user_linear,
    user_squares,
    item_factor,
    item_linear,
    item_squares,
):
    slot_count = ratings.shape[2]
    width = ratings.shape[3]
    rank = user_factor.shape[1]
    user_blocks = user_factor.shape[0] // width
    item_blocks = item_factor.shape[0] // width
    user_devices = lax.axis_size("users")
    tiles = (
        tile_user.reshape(slot_count),
        tile_item.reshape(slot_count),
        tile_count.reshape(1),
        ratings.reshape(slot_count, width, width),
        confidence.reshape(slot_count, width, width),
    )
    items = item_factor.reshape(item_blocks, width, rank)
    split = (user_blocks, width, rank)
    user_sum, item_sum = both_totals(
        tiles,
        user_linear.reshape(split),
        user_squares.reshape(split),
        user_factor.reshape(split),
        items,
        user_devices // (ALONG_Z * CORES),
        ALONG_Z,
    )
    user_grad = user_sum.reshape(user_blocks * width, rank) * width ** (-0.5)
    new_user_linear, new_user_squares = ftrl_state(
        user_grad, user_linear, user_squares, user_factor
    )
    new_user_factor = ftrl_factor(new_user_linear, new_user_squares)
    item_grad = item_sum * (width * user_devices) ** (-0.5)
    new_item_linear, new_item_squares = ftrl_state(
        item_grad, item_linear, item_squares, item_factor
    )
    new_item_factor = ftrl_factor(new_item_linear, new_item_squares)
    return (
        new_user_factor,
        new_user_linear,
        new_user_squares,
        new_item_factor,
        new_item_linear,
        new_item_squares,
    )


def solution(mesh):
    placed = (
        P("users", "items", None, None, None),
        P("users", "items", None, None, None),
        P("users", "items", None),
        P("users", "items", None),
        P("users", "items"),
        P("users", None),
        P("users", None),
        P("users", None),
        P("items", None),
        P("items", None),
        P("items", None),
    )
    return jax.shard_map(
        on_device,
        mesh=mesh,
        in_specs=placed,
        out_specs=(
            P("users", None),
            P("users", None),
            P("users", None),
            P("items", None),
            P("items", None),
            P("items", None),
        ),
        check_vma=False,
    )
```

```python
import functools

import jax
import jax.numpy as jnp
from jax import lax
from jax.experimental import pallas as pl
from jax.experimental.pallas import tpu as pltpu
from jax.sharding import PartitionSpec as P

learn_alpha = 0.25
beta_offset = 1.0
lasso_weight = 0.5
ridge_weight = 1.0

ALONG_Z = 12
CORES = 2


def ftrl_state(gradient, linear, squares, factor):
    new_squares = squares + gradient * gradient
    sigma_step = (jnp.sqrt(new_squares) - jnp.sqrt(squares)) / learn_alpha
    new_linear = linear + gradient - sigma_step * factor.astype(jnp.float32)
    return (new_linear, new_squares)


def ftrl_factor(linear, squares):
    shrink = linear - lasso_weight * jnp.sign(linear)
    denominator = (beta_offset + jnp.sqrt(squares)) / learn_alpha + ridge_weight
    weight = jnp.where(
        jnp.abs(linear) <= lasso_weight, jnp.zeros_like(linear), -shrink / denominator
    )
    return weight.astype(jnp.bfloat16)


def slot_table(tile_user, tile_item, item_blocks):
    return [tile_user[t] * item_blocks + tile_item[t] for t in range(tile_user.shape[0])]


def slot_of(codes, count, pair):
    slot = jnp.int32(0)
    live = jnp.int32(0)
    for t, code in enumerate(codes):
        slot = jnp.where(code == pair, t, slot)
        live = jnp.where(code == pair, jnp.where(t < count, 1, 0), live)
    return slot, live.astype(jnp.float32)


def pair_error(user_rows, item_rows, ratings, confidence, live):
    predict = lax.dot_general(
        user_rows, item_rows, (((1,), (1,)), ((), ())), preferred_element_type=jnp.float32
    )
    error = live * confidence.astype(jnp.float32) * (predict - ratings.astype(jnp.float32))
    return error.astype(jnp.bfloat16)


def remote(source, target, send, receive, device):
    return pltpu.make_async_remote_copy(
        src_ref=source,
        dst_ref=target,
        send_sem=send,
        recv_sem=receive,
        device_id=device,
        device_id_type=pl.DeviceIdType.MESH,
    )


def both_kernel(
    along_z,
    user_scale,
    tile_user,
    tile_item,
    tile_count,
    ratings_hbm,
    confidence_hbm,
    linear_hbm,
    squares_hbm,
    user_factor,
    item_factor,
    user_out,
    total,
    ratings,
    confidence,
    linear,
    squares,
    user_part,
    user_sum,
    fresh,
    pass_right,
    pass_left,
    from_left,
    from_right,
    part,
    arrived,
    mine,
    chunk_sum,
    first_in,
    tile_in,
    whole_in,
    load_sem,
    user_send,
    user_recv,
    send_swap,
    recv_swap,
    send_first,
    recv_first,
    send_second,
    recv_second,
    send_tile,
    recv_tile,
    send_chunk,
    recv_chunk,
    send_over,
    recv_over,
):
    user_blocks, width, rank = user_factor.shape
    item_blocks = item_factor.shape[0]
    half = width // 2
    quarter = width // 4
    half_rows = item_blocks * width // CORES
    along_y = lax.axis_size("users") // (along_z * CORES)
    user = lax.axis_index("users")
    core = lax.rem(user, CORES)
    z = lax.rem(user // CORES, along_z)
    y = user // (CORES * along_z)
    partner = {"users": user + 1 - 2 * core}
    n = lax.axis_size("items")
    me = lax.axis_index("items")
    right, left, far = lax.rem(me + 1, n), lax.rem(me + 3, n), lax.rem(me + 2, n)

    def at_y(t):
        return {"users": (t * along_z + z) * CORES + core}

    def at_z(t):
        return {"users": (y * along_z + t) * CORES + core}

    def greet(device):
        pl.semaphore_signal(
            barrier, inc=1, device_id=device, device_id_type=pl.DeviceIdType.MESH
        )

    barrier = pltpu.get_barrier_semaphore()
    loads = [
        pltpu.make_async_copy(ratings_hbm, ratings, load_sem.at[0]),
        pltpu.make_async_copy(confidence_hbm, confidence, load_sem.at[1]),
        pltpu.make_async_copy(linear_hbm, linear, load_sem.at[2]),
        pltpu.make_async_copy(squares_hbm, squares, load_sem.at[3]),
    ]
    loads[0].start()
    loads[1].start()
    greet({"items": left})
    greet({"items": right})
    greet(partner)

    @pl.loop(1, along_y)
    def _(d):
        greet(at_y(lax.rem(y + d, along_y)))

    @pl.loop(1, along_z)
    def _(d):
        greet(at_z(lax.rem(z + d, along_z)))

    codes = slot_table(tile_user, tile_item, item_blocks)
    count = tile_count[0]

    def user_block(k):
        rows = user_factor[k]
        gradient = jnp.zeros((width, rank), jnp.float32)
        for i in range(item_blocks):
            slot, live = slot_of(codes, count, k * item_blocks + i)
            error = pair_error(rows, item_factor[i], ratings[slot], confidence[slot], live)
            gradient += jnp.dot(error, item_factor[i], preferred_element_type=jnp.float32)
        user_part[k] = gradient

    def rows_at(start, size):
        return pl.ds(start, size)

    low, high = rows_at(0, half), rows_at(half, half)
    fours = [rows_at(q * quarter, quarter) for q in range(4)]
    to_right, to_left = {"items": right}, {"items": left}

    def user_copy(j, source, target, device):
        return remote(source, target, user_send.at[j], user_recv.at[j], device)

    far_right = user_copy(0, user_part.at[far, low], pass_right, to_right)
    far_left = user_copy(1, user_part.at[far, high], pass_left, to_left)
    near_right = user_copy(2, user_part.at[right, high], from_left.at[high], to_right)
    near_left = user_copy(3, user_part.at[left, low], from_right.at[low], to_left)
    sums_right = [
        user_copy(4 + q, user_part.at[right, fours[q]], from_left.at[fours[q]], to_right)
        for q in range(2)
    ]
    sums_left = [
        user_copy(4 + q, user_part.at[left, fours[q]], from_right.at[fours[q]], to_left)
        for q in range(2, 4)
    ]
    own_right = [
        user_copy(8 + q, user_sum.at[me, fours[q]], user_sum.at[me, fours[q]], to_right)
        for q in range(4)
    ]
    own_left = [
        user_copy(12 + q, user_sum.at[me, fours[q]], user_sum.at[me, fours[q]], to_left)
        for q in range(4)
    ]
    on_right = [
        user_copy(16 + q, user_sum.at[left, fours[q]], user_sum.at[left, fours[q]], to_right)
        for q in range(2)
    ]
    on_left = [
        user_copy(16 + q, user_sum.at[right, fours[q]], user_sum.at[right, fours[q]], to_left)
        for q in range(2, 4)
    ]

    loads[0].wait()
    loads[1].wait()
    loads[2].start()
    loads[3].start()
    user_block(far)
    pl.semaphore_wait(barrier, along_y + along_z + 1)
    far_right.start()
    far_left.start()
    user_block(right)
    near_right.start()
    user_block(left)
    near_left.start()
    far_right.wait_recv()
    for q in range(2):
        user_part[right, fours[q]] += pass_right[fours[q]]
        sums_right[q].start()
    far_left.wait_recv()
    for q in range(2, 4):
        user_part[left, fours[q]] += pass_left[fours[q - 2]]
        sums_left[q - 2].start()
    user_block(me)

    def own_sum(q):
        user_sum[me, fours[q]] = user_scale * (
            user_part[me, fours[q]] + (from_left[fours[q]] + from_right[fours[q]])
        )

    near_left.wait_recv()
    near_right.wait_recv()
    for q in range(2):
        sums_right[q].wait_recv()
        own_sum(q)
        own_right[q].start()
        sums_left[q].wait_recv()
        own_sum(2 + q)
        own_left[2 + q].start()
    for q in range(2):
        own_right[2 + q].start()
        own_left[q].start()
    loads[2].wait()
    loads[3].wait()

    def new_factor(k, start):
        slab = min(32, half)

        @pl.loop(0, half // slab)
        def _(j):
            rows = pl.ds(pl.multiple_of(start + j * slab, slab), slab)
            state, spread = ftrl_state(
                user_sum[k, rows, :], linear[k, rows, :], squares[k, rows, :], user_factor[k, rows, :]
            )
            shrink = state - jnp.where(state > 0.0, lasso_weight, -lasso_weight)
            denominator = (beta_offset + jnp.sqrt(spread)) / learn_alpha + ridge_weight
            weight = jnp.where(
                jnp.abs(state) <= lasso_weight, jnp.zeros_like(state), -shrink / denominator
            )
            fresh[k, rows, :] = weight.astype(jnp.bfloat16)

    def item_block(k, i, first=False):
        rows = pl.ds(pl.multiple_of(i * width, width), width)
        slot, live = slot_of(codes, count, k * item_blocks + i)
        error = pair_error(fresh[k], item_factor[i], ratings[slot], confidence[slot], live)
        gradient = lax.dot_general(
            error, fresh[k], (((0,), (0,)), ((), ())), preferred_element_type=jnp.float32
        )
        if first:
            part[rows, :] = gradient
        else:
            part[rows, :] += gradient

    new_factor(me, 0)
    new_factor(me, half)
    for q in range(2):
        own_right[q].wait_recv()
        on_right[q].start()
        own_left[2 + q].wait_recv()
        on_left[q].start()
    for i in range(item_blocks):
        item_block(me, i, first=True)
    new_factor(left, 0)
    new_factor(right, half)
    own_right[2].wait_recv()
    own_right[3].wait_recv()
    new_factor(left, half)
    for i in range(item_blocks):
        item_block(left, i)
    own_left[0].wait_recv()
    own_left[1].wait_recv()
    new_factor(right, 0)
    for i in range(item_blocks):
        item_block(right, i)
    for copy in on_right:
        copy.wait_recv()
    new_factor(far, 0)
    for copy in on_left:
        copy.wait_recv()
    new_factor(far, half)
    store = pltpu.make_async_copy(user_sum, user_out, load_sem.at[4])
    store.start()
    item_block(far, (item_blocks - 1) * (1 - core))
    item_block(far, 1)

    def distance(count, j):
        step = (j + 1) // 2
        return count // 2 + step * (1 - 2 * lax.rem(j, 2))

    def shifted(count, place, offset):
        return lax.rem(place + offset + count, count)

    def chunk_offset(count, j):
        reach = count // 4
        q = j - (2 * reach - 1)
        near = (1 + q // 2) * (2 * lax.rem(q + 2 * reach, 2) - 1)
        return jnp.where(
            j < reach,
            j - 2 * reach,
            jnp.where(
                j < 2 * reach - 1,
                3 * reach - 1 - j,
                jnp.where(j < count - 1, near, 0),
            ),
        )

    def swaps(base, count, place):
        chunk = half_rows // count

        def one(j):
            t = shifted(count, place, chunk_offset(count, j))
            return remote(
                part.at[pl.ds(pl.multiple_of(base + t * chunk, 8), chunk)],
                arrived.at[pl.ds(pl.multiple_of(t * chunk, 8), chunk)],
                send_swap.at[j],
                recv_swap.at[j],
                partner,
            )

        return one

    def halves(other, base, n_first, first, at_first, n_second, second, at_second, direct):
        chunk = half_rows // n_first
        to_partner = swaps(other, n_second, second)
        from_partner = swaps(base, n_first, first)

        @pl.loop(0, n_second)
        def _(j):
            to_partner(j).start()

        item_block(far, (item_blocks - 1) * (base // half_rows))

        def rows_of(t):
            return pl.ds(pl.multiple_of(t * chunk, 8), chunk)

        def out_rows(t):
            return pl.ds(pl.multiple_of(base + t * chunk, 8), chunk)

        def tile_of(t, start):
            return (
                pl.ds(pl.multiple_of(start + 8 * (t // 2), 8), 8),
                pl.ds(pl.multiple_of(128 * lax.rem(t, 2), 128), 128),
            )

        reach = n_first // 4

        def chunk_at(offset):
            return shifted(n_first, first, offset)

        def second_target(j):
            return lax.rem(second + distance(n_second, j), n_second)

        def to_first(j):
            offset = chunk_offset(n_first, j)
            hop = jnp.where(
                j < reach,
                j - reach,
                jnp.where(j < 2 * reach - 1, 2 * reach - 1 - j, offset),
            )
            return remote(
                mine.at[rows_of(chunk_at(offset))],
                first_in.at[j, pl.ds(0, chunk)],
                send_first.at[j],
                recv_first.at[j],
                at_first(chunk_at(hop)),
            )

        def to_second(j):
            t = second_target(j)
            return remote(
                chunk_sum.at[tile_of(t, 0)],
                tile_in.at[j],
                send_second.at[j],
                recv_second.at[j],
                at_second(t),
            )

        def whole_to(j):
            return remote(
                whole_in.at[second],
                whole_in.at[second],
                send_second.at[j],
                recv_second.at[j],
                at_second(second_target(j)),
            )

        my_tile = tile_of(second, base + first * chunk)

        def tile_out(j):
            return remote(
                total.at[my_tile],
                total.at[my_tile],
                send_tile.at[j],
                recv_tile.at[j],
                at_second(second_target(j)),
            )

        def spread(slot, owner, hop):
            rows = out_rows(chunk_at(owner))
            return remote(
                total.at[rows],
                total.at[rows],
                send_chunk.at[slot],
                recv_chunk.at[slot],
                at_first(chunk_at(hop)),
            )

        def near_hop(j):
            return (reach - j // 2) * (2 * lax.rem(j, 2) - 1)

        def near_out(j):
            return spread(j, 0, near_hop(j))

        def on_down(j):
            return spread(2 * reach + j, reach, j - reach)

        def on_up(j):
            return spread(3 * reach + j, -reach, reach - 1 - j)

        def over(slot, t):
            return remote(
                total.at[out_rows(t)],
                total.at[out_rows(t)],
                send_over.at[slot],
                recv_over.at[slot],
                partner,
            )

        def swapped(j):
            from_partner(j).wait_recv()
            t = chunk_at(chunk_offset(n_first, j))
            return part[out_rows(t), :] + arrived[rows_of(t), :]

        @pl.loop(0, n_first - 3)
        def _(j):
            mine[rows_of(chunk_at(chunk_offset(n_first, j))), :] = swapped(j)
            to_first(j).start()

        def add_first(j, running):
            to_first(j).wait_recv()
            return running + first_in[j, pl.ds(0, chunk), :]

        down, up = n_first - 3, n_first - 2
        mine[rows_of(chunk_at(-reach)), :] = lax.fori_loop(0, reach, add_first, swapped(down))
        to_first(down).start()
        mine[rows_of(chunk_at(reach)), :] = lax.fori_loop(
            reach, 2 * reach - 1, add_first, swapped(up)
        )
        to_first(up).start()
        near = lax.fori_loop(2 * reach - 1, n_first - 1, add_first, swapped(n_first - 1))

        if direct:
            whole_in[second] = near

            @pl.loop(0, n_second - 1)
            def _(j):
                whole_to(j).start()

            @pl.loop(0, n_second - 1)
            def _(j):
                whole_to(j).wait_recv()

            total[out_rows(first), :] = lax.fori_loop(
                1, n_second, lambda j, running: running + whole_in[j], whole_in[0]
            )
        else:
            chunk_sum[...] = near

            @pl.loop(0, n_second - 1)
            def _(j):
                to_second(j).start()

            def add_second(j, running):
                to_second(j).wait_recv()
                return running + tile_in[j]

            total[my_tile] = lax.fori_loop(
                0, n_second - 1, add_second, chunk_sum[tile_of(second, 0)]
            )

            @pl.loop(0, n_second - 1)
            def _(j):
                tile_out(j).start()

            @pl.loop(0, n_second - 1)
            def _(j):
                tile_out(j).wait_recv()

        @pl.loop(0, 2 * reach)
        def _(j):
            near_out(j).start()

        over(n_first - 1, first).start()

        near_out(0).wait_recv()

        @pl.loop(0, reach)
        def _(j):
            on_down(j).start()

        near_out(1).wait_recv()

        @pl.loop(0, reach - 1)
        def _(j):
            on_up(j).start()

        over(0, chunk_at(reach)).start()
        over(1, chunk_at(-reach)).start()

        @pl.loop(2, 2 * reach)
        def _(j):
            near_out(j).wait_recv()
            over(j, chunk_at(-near_hop(j))).start()

        @pl.loop(0, reach)
        def _(j):
            on_down(j).wait_recv()
            over(2 * reach + j, chunk_at(2 * reach - j)).start()

        @pl.loop(0, reach - 1)
        def _(j):
            on_up(j).wait_recv()
            over(3 * reach + j, chunk_at(1 + j - 2 * reach)).start()

        @pl.loop(0, n_first - 1)
        def _(j):
            to_first(j).wait_send()

        @pl.loop(0, 2 * reach)
        def _(j):
            near_out(j).wait_send()

        @pl.loop(0, reach)
        def _(j):
            on_down(j).wait_send()

        @pl.loop(0, reach - 1)
        def _(j):
            on_up(j).wait_send()

        @pl.loop(0, n_second - 1)
        def _(j):
            if direct:
                whole_to(j).wait_send()
            else:
                to_second(j).wait_send()
                tile_out(j).wait_send()

        @pl.loop(0, n_first)
        def _(j):
            over(j, 0).wait_send()

        @pl.loop(0, n_second)
        def _(j):
            to_partner(j).wait_send()

        other_chunk = half_rows // n_second

        @pl.loop(0, n_second)
        def _(j):
            remote(
                total.at[pl.ds(0, other_chunk)],
                total.at[pl.ds(0, other_chunk)],
                send_over.at[j],
                recv_over.at[j],
                partner,
            ).wait_recv()

    @pl.when(core == 0)
    def _():
        halves(half_rows, 0, along_y, y, at_y, along_z, z, at_z, False)

    @pl.when(core == 1)
    def _():
        halves(0, half_rows, along_z, z, at_z, along_y, y, at_y, True)

    for copy in [far_right, far_left, near_right, near_left] + sums_right + sums_left:
        copy.wait_send()
    for copy in own_right + own_left + on_right + on_left:
        copy.wait_send()
    store.wait()


VMEM = pl.BlockSpec(memory_space=pltpu.VMEM)
SMEM = pl.BlockSpec(memory_space=pltpu.SMEM)
ANY = pl.BlockSpec(memory_space=pl.ANY)
DMA = pltpu.SemaphoreType.DMA


def both_totals(tiles, linear, squares, user_factor, item_factor, along_y, along_z):
    blocks, width, rank = user_factor.shape
    rows = item_factor.shape[0] * width
    half_rows = rows // CORES
    most = max(along_y, along_z)
    chunk_y, chunk_z = half_rows // along_y, half_rows // along_z
    chunk = max(chunk_y, chunk_z)
    f32 = jnp.float32
    whole = (blocks, width, rank)
    return pl.pallas_call(
        functools.partial(both_kernel, along_z, width ** (-0.5)),
        name="both_totals",
        out_shape=(jax.ShapeDtypeStruct(whole, f32), jax.ShapeDtypeStruct((rows, rank), f32)),
        in_specs=[SMEM] * 3 + [ANY] * 4 + [VMEM] * 2,
        out_specs=(ANY, VMEM),
        scratch_shapes=[
            pltpu.VMEM(tiles[3].shape, tiles[3].dtype),
            pltpu.VMEM(tiles[4].shape, tiles[4].dtype),
            pltpu.VMEM(whole, f32),
            pltpu.VMEM(whole, f32),
            pltpu.VMEM(whole, f32),
            pltpu.VMEM(whole, f32),
            pltpu.VMEM(whole, user_factor.dtype),
            pltpu.VMEM((width // 2, rank), f32),
            pltpu.VMEM((width // 2, rank), f32),
            pltpu.VMEM((width, rank), f32),
            pltpu.VMEM((width, rank), f32),
            pltpu.VMEM((rows, rank), f32),
            pltpu.VMEM((half_rows, rank), f32),
            pltpu.VMEM((half_rows, rank), f32),
            pltpu.VMEM((chunk_y, rank), f32),
            pltpu.VMEM((most - 1, chunk, rank), f32),
            pltpu.VMEM((most - 1, 8, 128), f32),
            pltpu.VMEM((along_y, chunk_z, rank), f32),
            DMA((5,)),
            DMA((20,)),
            DMA((20,)),
        ]
        + [DMA((most,))] * 12,
        compiler_params=pltpu.CompilerParams(collective_id=0, has_side_effects=True),
    )(*tiles, linear, squares, user_factor, item_factor)


def on_device(
    ratings,
    confidence,
    tile_user,
    tile_item,
    tile_count,
    user_factor,
    user_linear,
    user_squares,
    item_factor,
    item_linear,
    item_squares,
):
    slot_count = ratings.shape[2]
    width = ratings.shape[3]
    rank = user_factor.shape[1]
    user_blocks = user_factor.shape[0] // width
    item_blocks = item_factor.shape[0] // width
    user_devices = lax.axis_size("users")
    tiles = (
        tile_user.reshape(slot_count),
        tile_item.reshape(slot_count),
        tile_count.reshape(1),
        ratings.reshape(slot_count, width, width),
        confidence.reshape(slot_count, width, width),
    )
    items = item_factor.reshape(item_blocks, width, rank)
    split = (user_blocks, width, rank)
    user_sum, item_sum = both_totals(
        tiles,
        user_linear.reshape(split),
        user_squares.reshape(split),
        user_factor.reshape(split),
        items,
        user_devices // (ALONG_Z * CORES),
        ALONG_Z,
    )
    user_grad = user_sum.reshape(user_blocks * width, rank)
    new_user_linear, new_user_squares = ftrl_state(
        user_grad, user_linear, user_squares, user_factor
    )
    new_user_factor = ftrl_factor(new_user_linear, new_user_squares)
    item_grad = item_sum * (width * user_devices) ** (-0.5)
    new_item_linear, new_item_squares = ftrl_state(
        item_grad, item_linear, item_squares, item_factor
    )
    new_item_factor = ftrl_factor(new_item_linear, new_item_squares)
    return (
        new_user_factor,
        new_user_linear,
        new_user_squares,
        new_item_factor,
        new_item_linear,
        new_item_squares,
    )


def solution(mesh):
    placed = (
        P("users", "items", None, None, None),
        P("users", "items", None, None, None),
        P("users", "items", None),
        P("users", "items", None),
        P("users", "items"),
        P("users", None),
        P("users", None),
        P("users", None),
        P("items", None),
        P("items", None),
        P("items", None),
    )
    return jax.shard_map(
        on_device,
        mesh=mesh,
        in_specs=placed,
        out_specs=(
            P("users", None),
            P("users", None),
            P("users", None),
            P("items", None),
            P("items", None),
            P("items", None),
        ),
        check_vma=False,
    )
```

```python
import functools

import jax
import jax.numpy as jnp
from jax import lax
from jax.experimental import pallas as pl
from jax.experimental.pallas import tpu as pltpu
from jax.sharding import PartitionSpec as P

learn_alpha = 0.25
beta_offset = 1.0
lasso_weight = 0.5
ridge_weight = 1.0

ALONG_Z = 12
CORES = 2


def ftrl_state(gradient, linear, squares, factor):
    new_squares = squares + gradient * gradient
    sigma_step = (jnp.sqrt(new_squares) - jnp.sqrt(squares)) / learn_alpha
    new_linear = linear + gradient - sigma_step * factor.astype(jnp.float32)
    return (new_linear, new_squares)


def ftrl_factor(linear, squares):
    shrink = linear - lasso_weight * jnp.sign(linear)
    denominator = (beta_offset + jnp.sqrt(squares)) / learn_alpha + ridge_weight
    weight = jnp.where(
        jnp.abs(linear) <= lasso_weight, jnp.zeros_like(linear), -shrink / denominator
    )
    return weight.astype(jnp.bfloat16)


def slot_table(tile_user, tile_item, item_blocks):
    return [tile_user[t] * item_blocks + tile_item[t] for t in range(tile_user.shape[0])]


def slot_of(codes, count, pair):
    slot = jnp.int32(0)
    live = jnp.int32(0)
    for t, code in enumerate(codes):
        slot = jnp.where(code == pair, t, slot)
        live = jnp.where(code == pair, jnp.where(t < count, 1, 0), live)
    return slot, live.astype(jnp.float32)


def pair_error(user_rows, item_rows, ratings, confidence, live):
    predict = lax.dot_general(
        user_rows, item_rows, (((1,), (1,)), ((), ())), preferred_element_type=jnp.float32
    )
    error = live * confidence.astype(jnp.float32) * (predict - ratings.astype(jnp.float32))
    return error.astype(jnp.bfloat16)


def remote(source, target, send, receive, device):
    return pltpu.make_async_remote_copy(
        src_ref=source,
        dst_ref=target,
        send_sem=send,
        recv_sem=receive,
        device_id=device,
        device_id_type=pl.DeviceIdType.MESH,
    )


def both_kernel(
    along_z,
    user_scale,
    tile_user,
    tile_item,
    tile_count,
    ratings_hbm,
    confidence_hbm,
    linear_hbm,
    squares_hbm,
    user_factor,
    item_factor,
    user_out,
    total,
    ratings,
    confidence,
    linear,
    squares,
    user_part,
    user_sum,
    fresh,
    pass_right,
    pass_left,
    from_left,
    from_right,
    part,
    arrived,
    mine,
    chunk_sum,
    first_in,
    tile_in,
    whole_in,
    load_sem,
    user_send,
    user_recv,
    send_swap,
    recv_swap,
    send_first,
    recv_first,
    send_second,
    recv_second,
    send_tile,
    recv_tile,
    send_chunk,
    recv_chunk,
    send_over,
    recv_over,
):
    user_blocks, width, rank = user_factor.shape
    item_blocks = item_factor.shape[0]
    half = width // 2
    quarter = width // 4
    half_rows = item_blocks * width // CORES
    along_y = lax.axis_size("users") // (along_z * CORES)
    user = lax.axis_index("users")
    core = lax.rem(user, CORES)
    z = lax.rem(user // CORES, along_z)
    y = user // (CORES * along_z)
    partner = {"users": user + 1 - 2 * core}
    n = lax.axis_size("items")
    me = lax.axis_index("items")
    right, left, far = lax.rem(me + 1, n), lax.rem(me + 3, n), lax.rem(me + 2, n)

    def at_y(t):
        return {"users": (t * along_z + z) * CORES + core}

    def at_z(t):
        return {"users": (y * along_z + t) * CORES + core}

    def greet(device):
        pl.semaphore_signal(
            barrier, inc=1, device_id=device, device_id_type=pl.DeviceIdType.MESH
        )

    barrier = pltpu.get_barrier_semaphore()
    loads = [
        pltpu.make_async_copy(ratings_hbm, ratings, load_sem.at[0]),
        pltpu.make_async_copy(confidence_hbm, confidence, load_sem.at[1]),
        pltpu.make_async_copy(linear_hbm, linear, load_sem.at[2]),
        pltpu.make_async_copy(squares_hbm, squares, load_sem.at[3]),
    ]
    loads[0].start()
    loads[1].start()
    greet({"items": left})
    greet({"items": right})
    greet(partner)

    @pl.loop(1, along_y)
    def _(d):
        greet(at_y(lax.rem(y + d, along_y)))

    @pl.loop(1, along_z)
    def _(d):
        greet(at_z(lax.rem(z + d, along_z)))

    codes = slot_table(tile_user, tile_item, item_blocks)
    count = tile_count[0]

    def user_block(k):
        rows = user_factor[k]
        gradient = jnp.zeros((width, rank), jnp.float32)
        for i in range(item_blocks):
            slot, live = slot_of(codes, count, k * item_blocks + i)
            error = pair_error(rows, item_factor[i], ratings[slot], confidence[slot], live)
            gradient += jnp.dot(error, item_factor[i], preferred_element_type=jnp.float32)
        user_part[k] = gradient

    def rows_at(start, size):
        return pl.ds(start, size)

    low, high = rows_at(0, half), rows_at(half, half)
    fours = [rows_at(q * quarter, quarter) for q in range(4)]
    to_right, to_left = {"items": right}, {"items": left}

    def user_copy(j, source, target, device):
        return remote(source, target, user_send.at[j], user_recv.at[j], device)

    far_right = user_copy(0, user_part.at[far, low], pass_right, to_right)
    far_left = user_copy(1, user_part.at[far, high], pass_left, to_left)
    near_right = user_copy(2, user_part.at[right, high], from_left.at[high], to_right)
    near_left = user_copy(3, user_part.at[left, low], from_right.at[low], to_left)
    sums_right = [
        user_copy(4 + q, user_part.at[right, fours[q]], from_left.at[fours[q]], to_right)
        for q in range(2)
    ]
    sums_left = [
        user_copy(4 + q, user_part.at[left, fours[q]], from_right.at[fours[q]], to_left)
        for q in range(2, 4)
    ]
    own_right = [
        user_copy(8 + q, user_sum.at[me, fours[q]], user_sum.at[me, fours[q]], to_right)
        for q in range(4)
    ]
    own_left = [
        user_copy(12 + q, user_sum.at[me, fours[q]], user_sum.at[me, fours[q]], to_left)
        for q in range(4)
    ]
    on_right = [
        user_copy(16 + q, user_sum.at[left, fours[q]], user_sum.at[left, fours[q]], to_right)
        for q in range(2)
    ]
    on_left = [
        user_copy(16 + q, user_sum.at[right, fours[q]], user_sum.at[right, fours[q]], to_left)
        for q in range(2, 4)
    ]

    loads[0].wait()
    loads[1].wait()
    loads[2].start()
    loads[3].start()
    user_block(far)
    pl.semaphore_wait(barrier, along_y + along_z + 1)
    far_right.start()
    far_left.start()
    user_block(right)
    near_right.start()
    user_block(left)
    near_left.start()
    far_right.wait_recv()
    for q in range(2):
        user_part[right, fours[q]] += pass_right[fours[q]]
        sums_right[q].start()
    far_left.wait_recv()
    for q in range(2, 4):
        user_part[left, fours[q]] += pass_left[fours[q - 2]]
        sums_left[q - 2].start()
    user_block(me)

    def own_sum(q):
        user_sum[me, fours[q]] = user_scale * (
            user_part[me, fours[q]] + (from_left[fours[q]] + from_right[fours[q]])
        )

    near_left.wait_recv()
    near_right.wait_recv()
    for q in range(2):
        sums_right[q].wait_recv()
        own_sum(q)
        own_right[q].start()
        sums_left[q].wait_recv()
        own_sum(2 + q)
        own_left[2 + q].start()
    for q in range(2):
        own_right[2 + q].start()
        own_left[q].start()
    loads[2].wait()
    loads[3].wait()

    def new_factor(k, start):
        slab = min(32, half)

        @pl.loop(0, half // slab)
        def _(j):
            rows = pl.ds(pl.multiple_of(start + j * slab, slab), slab)
            state, spread = ftrl_state(
                user_sum[k, rows, :], linear[k, rows, :], squares[k, rows, :], user_factor[k, rows, :]
            )
            shrink = state - jnp.where(state > 0.0, lasso_weight, -lasso_weight)
            denominator = (beta_offset + jnp.sqrt(spread)) / learn_alpha + ridge_weight
            weight = jnp.where(
                jnp.abs(state) <= lasso_weight, jnp.zeros_like(state), -shrink / denominator
            )
            fresh[k, rows, :] = weight.astype(jnp.bfloat16)

    def item_block(k, i, first=False):
        rows = pl.ds(pl.multiple_of(i * width, width), width)
        slot, live = slot_of(codes, count, k * item_blocks + i)
        error = pair_error(fresh[k], item_factor[i], ratings[slot], confidence[slot], live)
        gradient = lax.dot_general(
            error, fresh[k], (((0,), (0,)), ((), ())), preferred_element_type=jnp.float32
        )
        if first:
            part[rows, :] = gradient
        else:
            part[rows, :] += gradient

    new_factor(me, 0)
    new_factor(me, half)
    for q in range(2):
        own_right[q].wait_recv()
        on_right[q].start()
        own_left[2 + q].wait_recv()
        on_left[q].start()
    for i in range(item_blocks):
        item_block(me, i, first=True)
    new_factor(left, 0)
    new_factor(right, half)
    own_right[2].wait_recv()
    own_right[3].wait_recv()
    new_factor(left, half)
    for i in range(item_blocks):
        item_block(left, i)
    own_left[0].wait_recv()
    own_left[1].wait_recv()
    new_factor(right, 0)
    for i in range(item_blocks):
        item_block(right, i)
    for copy in on_right:
        copy.wait_recv()
    new_factor(far, 0)
    for copy in on_left:
        copy.wait_recv()
    new_factor(far, half)
    store = pltpu.make_async_copy(user_sum, user_out, load_sem.at[4])
    store.start()
    item_block(far, (item_blocks - 1) * (1 - core))
    item_block(far, 1)

    def distance(count, j):
        step = (j + 1) // 2
        return count // 2 + step * (1 - 2 * lax.rem(j, 2))

    def swaps(base, count, place):
        chunk = half_rows // count

        def one(j):
            t = lax.rem(place + distance(count, j), count)
            return remote(
                part.at[pl.ds(pl.multiple_of(base + t * chunk, 8), chunk)],
                arrived.at[pl.ds(pl.multiple_of(t * chunk, 8), chunk)],
                send_swap.at[j],
                recv_swap.at[j],
                partner,
            )

        return one

    def halves(other, base, n_first, first, at_first, n_second, second, at_second, direct):
        chunk = half_rows // n_first
        to_partner = swaps(other, n_second, second)
        from_partner = swaps(base, n_first, first)

        @pl.loop(0, n_second)
        def _(j):
            to_partner(j).start()

        item_block(far, (item_blocks - 1) * (base // half_rows))

        def rows_of(t):
            return pl.ds(pl.multiple_of(t * chunk, 8), chunk)

        def out_rows(t):
            return pl.ds(pl.multiple_of(base + t * chunk, 8), chunk)

        def tile_of(t, start):
            return (
                pl.ds(pl.multiple_of(start + 8 * (t // 2), 8), 8),
                pl.ds(pl.multiple_of(128 * lax.rem(t, 2), 128), 128),
            )

        def first_target(j):
            return lax.rem(first + distance(n_first, j), n_first)

        def second_target(j):
            return lax.rem(second + distance(n_second, j), n_second)

        columns = [pl.ds(0, rank // 2), pl.ds(rank // 2, rank // 2)]
        most = first_in.shape[0]

        def to_first(h, j):
            t = first_target(j)
            return remote(
                mine.at[rows_of(t), columns[h]],
                first_in.at[j, pl.ds(0, chunk), columns[h]],
                send_first.at[h * most + j],
                recv_first.at[h * most + j],
                at_first(t),
            )

        def to_second(j):
            t = second_target(j)
            return remote(
                chunk_sum.at[tile_of(t, 0)],
                tile_in.at[j],
                send_second.at[j],
                recv_second.at[j],
                at_second(t),
            )

        def whole_to(h, j):
            return remote(
                whole_in.at[second, :, columns[h]],
                whole_in.at[second, :, columns[h]],
                send_second.at[h * most + j],
                recv_second.at[h * most + j],
                at_second(second_target(j)),
            )

        my_tile = tile_of(second, base + first * chunk)

        def tile_out(j):
            return remote(
                total.at[my_tile],
                total.at[my_tile],
                send_tile.at[j],
                recv_tile.at[j],
                at_second(second_target(j)),
            )

        def chunk_out(h, j):
            return remote(
                total.at[out_rows(first), columns[h]],
                total.at[out_rows(first), columns[h]],
                send_chunk.at[h * most + j],
                recv_chunk.at[h * most + j],
                at_first(first_target(j)),
            )

        def over(slot, t):
            return remote(
                total.at[out_rows(t)],
                total.at[out_rows(t)],
                send_over.at[slot],
                recv_over.at[slot],
                partner,
            )

        @pl.loop(0, n_first - 1)
        def _(j):
            from_partner(j).wait_recv()
            t = first_target(j)
            mine[rows_of(t), :] = part[out_rows(t), :] + arrived[rows_of(t), :]
            to_first(0, j).start()

        @pl.loop(0, n_first - 1)
        def _(j):
            to_first(1, j).start()

        from_partner(n_first - 1).wait_recv()

        def near(h):
            def add_first(j, running):
                to_first(h, j).wait_recv()
                return running + first_in[j, pl.ds(0, chunk), columns[h]]

            return lax.fori_loop(
                0,
                n_first - 1,
                add_first,
                part[out_rows(first), columns[h]] + arrived[rows_of(first), columns[h]],
            )

        def start_chunks(h):
            @pl.loop(0, n_first - 1)
            def _(j):
                chunk_out(h, j).start()

        if direct:
            for h in range(2):
                whole_in[second, :, columns[h]] = near(h)

                @pl.loop(0, n_second - 1)
                def _(j):
                    whole_to(h, j).start()

            for h in range(2):

                @pl.loop(0, n_second - 1)
                def _(j):
                    whole_to(h, j).wait_recv()

                total[out_rows(first), columns[h]] = lax.fori_loop(
                    1,
                    n_second,
                    lambda j, running: running + whole_in[j, :, columns[h]],
                    whole_in[0, :, columns[h]],
                )
                start_chunks(h)
        else:
            def in_half(h, j):
                return lax.rem(second_target(j), 2) == h

            for h in range(2):
                chunk_sum[:, columns[h]] = near(h)

                @pl.loop(0, n_second - 1)
                def _(j):
                    @pl.when(in_half(h, j))
                    def _():
                        to_second(j).start()

            def add_second(j, running):
                to_second(j).wait_recv()
                return running + tile_in[j]

            total[my_tile] = lax.fori_loop(
                0, n_second - 1, add_second, chunk_sum[tile_of(second, 0)]
            )

            @pl.loop(0, n_second - 1)
            def _(j):
                tile_out(j).start()

            for h in range(2):

                @pl.loop(0, n_second - 1)
                def _(j):
                    @pl.when(in_half(h, j))
                    def _():
                        tile_out(j).wait_recv()

                start_chunks(h)

        over(n_first - 1, first).start()

        @pl.loop(0, n_first - 1)
        def _(j):
            chunk_out(0, j).wait_recv()
            chunk_out(1, j).wait_recv()
            over(j, lax.rem(first + n_first - distance(n_first, j), n_first)).start()

        for h in range(2):

            @pl.loop(0, n_first - 1)
            def _(j):
                to_first(h, j).wait_send()
                chunk_out(h, j).wait_send()

        @pl.loop(0, n_second - 1)
        def _(j):
            if direct:
                whole_to(0, j).wait_send()
                whole_to(1, j).wait_send()
            else:
                to_second(j).wait_send()
                tile_out(j).wait_send()

        @pl.loop(0, n_first)
        def _(j):
            over(j, 0).wait_send()

        @pl.loop(0, n_second)
        def _(j):
            to_partner(j).wait_send()

        other_chunk = half_rows // n_second

        @pl.loop(0, n_second)
        def _(j):
            remote(
                total.at[pl.ds(0, other_chunk)],
                total.at[pl.ds(0, other_chunk)],
                send_over.at[j],
                recv_over.at[j],
                partner,
            ).wait_recv()

    @pl.when(core == 0)
    def _():
        halves(half_rows, 0, along_y, y, at_y, along_z, z, at_z, False)

    @pl.when(core == 1)
    def _():
        halves(0, half_rows, along_z, z, at_z, along_y, y, at_y, True)

    for copy in [far_right, far_left, near_right, near_left] + sums_right + sums_left:
        copy.wait_send()
    for copy in own_right + own_left + on_right + on_left:
        copy.wait_send()
    store.wait()


VMEM = pl.BlockSpec(memory_space=pltpu.VMEM)
SMEM = pl.BlockSpec(memory_space=pltpu.SMEM)
ANY = pl.BlockSpec(memory_space=pl.ANY)
DMA = pltpu.SemaphoreType.DMA


def both_totals(tiles, linear, squares, user_factor, item_factor, along_y, along_z):
    blocks, width, rank = user_factor.shape
    rows = item_factor.shape[0] * width
    half_rows = rows // CORES
    most = max(along_y, along_z)
    chunk_y, chunk_z = half_rows // along_y, half_rows // along_z
    chunk = max(chunk_y, chunk_z)
    f32 = jnp.float32
    whole = (blocks, width, rank)
    return pl.pallas_call(
        functools.partial(both_kernel, along_z, width ** (-0.5)),
        name="both_totals",
        out_shape=(jax.ShapeDtypeStruct(whole, f32), jax.ShapeDtypeStruct((rows, rank), f32)),
        in_specs=[SMEM] * 3 + [ANY] * 4 + [VMEM] * 2,
        out_specs=(ANY, VMEM),
        scratch_shapes=[
            pltpu.VMEM(tiles[3].shape, tiles[3].dtype),
            pltpu.VMEM(tiles[4].shape, tiles[4].dtype),
            pltpu.VMEM(whole, f32),
            pltpu.VMEM(whole, f32),
            pltpu.VMEM(whole, f32),
            pltpu.VMEM(whole, f32),
            pltpu.VMEM(whole, user_factor.dtype),
            pltpu.VMEM((width // 2, rank), f32),
            pltpu.VMEM((width // 2, rank), f32),
            pltpu.VMEM((width, rank), f32),
            pltpu.VMEM((width, rank), f32),
            pltpu.VMEM((rows, rank), f32),
            pltpu.VMEM((half_rows, rank), f32),
            pltpu.VMEM((half_rows, rank), f32),
            pltpu.VMEM((chunk_y, rank), f32),
            pltpu.VMEM((most, chunk, rank), f32),
            pltpu.VMEM((most - 1, 8, 128), f32),
            pltpu.VMEM((along_y, chunk_z, rank), f32),
            DMA((5,)),
            DMA((20,)),
            DMA((20,)),
        ]
        + [DMA((2 * most,))] * 12,
        compiler_params=pltpu.CompilerParams(collective_id=0, has_side_effects=True),
    )(*tiles, linear, squares, user_factor, item_factor)


def on_device(
    ratings,
    confidence,
    tile_user,
    tile_item,
    tile_count,
    user_factor,
    user_linear,
    user_squares,
    item_factor,
    item_linear,
    item_squares,
):
    slot_count = ratings.shape[2]
    width = ratings.shape[3]
    rank = user_factor.shape[1]
    user_blocks = user_factor.shape[0] // width
    item_blocks = item_factor.shape[0] // width
    user_devices = lax.axis_size("users")
    tiles = (
        tile_user.reshape(slot_count),
        tile_item.reshape(slot_count),
        tile_count.reshape(1),
        ratings.reshape(slot_count, width, width),
        confidence.reshape(slot_count, width, width),
    )
    items = item_factor.reshape(item_blocks, width, rank)
    split = (user_blocks, width, rank)
    user_sum, item_sum = both_totals(
        tiles,
        user_linear.reshape(split),
        user_squares.reshape(split),
        user_factor.reshape(split),
        items,
        user_devices // (ALONG_Z * CORES),
        ALONG_Z,
    )
    user_grad = user_sum.reshape(user_blocks * width, rank)
    new_user_linear, new_user_squares = ftrl_state(
        user_grad, user_linear, user_squares, user_factor
    )
    new_user_factor = ftrl_factor(new_user_linear, new_user_squares)
    item_grad = item_sum * (width * user_devices) ** (-0.5)
    new_item_linear, new_item_squares = ftrl_state(
        item_grad, item_linear, item_squares, item_factor
    )
    new_item_factor = ftrl_factor(new_item_linear, new_item_squares)
    return (
        new_user_factor,
        new_user_linear,
        new_user_squares,
        new_item_factor,
        new_item_linear,
        new_item_squares,
    )


def solution(mesh):
    placed = (
        P("users", "items", None, None, None),
        P("users", "items", None, None, None),
        P("users", "items", None),
        P("users", "items", None),
        P("users", "items"),
        P("users", None),
        P("users", None),
        P("users", None),
        P("items", None),
        P("items", None),
        P("items", None),
    )
    return jax.shard_map(
        on_device,
        mesh=mesh,
        in_specs=placed,
        out_specs=(
            P("users", None),
            P("users", None),
            P("users", None),
            P("items", None),
            P("items", None),
            P("items", None),
        ),
        check_vma=False,
    )
```
